128 devices in a mesh: gx: 16 (over x, y_hi, core), gy: 8 (over y_lo, z).
Axes of the slice: x: 4, y: 4 (y_hi: 2, y_lo: 2; y = y_hi * 2 + y_lo), z: 4, core: 2. Of those that a mesh axis runs over, the one named last changes fastest.
Arguments:
- populations: float32 [19, 256, 128, 128], P(None, 'gx', 'gy'), may hold values from 0.5 to 1.5
- coarse_state: float32 [4, 128, 64, 64], P(None, 'gx', 'gy'), may hold values from -3 to 3
- window_shift: int32 [1], replicated, may hold values from 1 to 15
- inflow: float32 [3], replicated, may hold values from -0.2 to 0.2
- relaxation: float32 [1], replicated, may hold values from 1 to 1.7
- positions: float32 [2048, 3, 642], P(('gx', 'gy')), may hold values from 0.25 to 6.75
- rest_shape: float32 [3, 642], replicated, may hold values from -6 to 6
- stiffness: float32 [2048], P(('gx', 'gy')), may hold values from 0.1 to 1
- cell_owner: int32 [2048, 1], P(('gx', 'gy')), may hold values from 0 to 15; in each aligned block of 16 rows (0 to 15, 16 to 31, ...) at most 2 rows name the same one
- cell_block: int32 [2048], P(('gx', 'gy')), may hold values from 0 to 63
- triangles: int32 [1280, 3], replicated, may hold values from 0 to 641, as said below
Outputs:
- flow: float32 [19, 256, 128, 128], P(None, 'gx', 'gy')
- cell_velocity: float32 [2048, 3, 642], P(('gx', 'gy'))
The draws below stay inside these ranges and needn't reach their ends.
Inputs may be any that keep to these rules, and one draw needn't show every extreme that they name: `triangles`: each triangle names three different vertices. `cell_owner`: among the cells of one device, no owner is named by more than 2 cells.
All inputs are finite; a program needn't handle non-finite values.
Results may differ from the reference program's by a relative error of at most 0.0003.
Values sent between devices are 32-bit elements; how exact they have to be, the bound alone decides.
No kernel may reach another device: no remote copies, remote signals or barrier semaphores. Data moves between devices by JAX's collectives and lax.ppermute only.
A program may use at most 128 MiB of HBM per device.

```python
import math
import jax
import jax.numpy as jnp
import numpy as np
from jax import lax

Q = 19
BS = 8
CX = 16
CY = 16
CZ = 128
V = 642
NTRI = 1280
CELLS_DEV = 16
CAP = 2
NB_DEV = 64
NX = 256
NY = 128
NZ = 128
CELLS = 2048
N_GX = 16
N_GY = 8


def draw_triangles(key, part):
    first_key, second_key, third_key = jax.random.split(jax.random.fold_in(key, 17), 3)
    first = jax.random.randint(first_key, (NTRI,), 0, V)
    offset_near = jax.random.randint(second_key, (NTRI,), 1, V // 2)
    offset_far = jax.random.randint(third_key, (NTRI,), V // 2, V)
    return jnp.stack([first, (first + offset_near) % V, (first + offset_far) % V], 1).astype(jnp.int32)


def touch_ends(entries, key, least, largest):
    longest = entries.shape.index(max(entries.shape))
    spots = []
    for shift in (0, 1):
        where = [jax.random.randint(jax.random.fold_in(key, axis), (), 0, length) for axis, length in enumerate(entries.shape)]
        where[longest] = (where[longest] + shift) % entries.shape[longest]
        spots.append(tuple(where))
    return entries.at[spots[0]].set(least).at[spots[1]].set(largest)


def steps_of(rng, shape, shards, smallest, largest):
    def one(dim, shards_of):
        steps = jax.random.uniform(jax.random.fold_in(jax.random.fold_in(rng, 6), dim), (shards_of,), jnp.float32, smallest / len(shards), largest / len(shards))
        return jnp.repeat(jnp.exp(steps), shape[dim] // shards_of).reshape((-1,) + (1,) * (len(shape) - dim - 1))

    gain = one(*shards[0])
    for cut in shards[1:]:
        gain = gain * one(*cut)
    return gain


def deal_out(key, own, number, rows, number_of, top, bound, skew):
    sequence = jax.random.permutation(key, number_of)
    crowded, common = shares(number_of, rows * top, bound, skew, True), shares(number_of, rows * top, bound, skew, False)
    places = jnp.arange(number_of)

    def named(lengths, turn):
        used = int((lengths > 0).sum())
        fixed = max(1, used // 4)
        shifted = fixed + (places - fixed + turn * (used - fixed)) % max(1, number_of - fixed)
        return jnp.zeros((number_of,), jnp.int32).at[sequence[jnp.where(places < fixed, places, shifted)]].set(jnp.asarray(lengths, jnp.int32))

    lengths = jnp.where(number % 4 == 0, named(crowded, number // 4), named(common, number - number // 4 - 1))
    mixed = jax.random.permutation(jax.random.fold_in(own, 3), number_of)
    source_of, sink = mixed[0:number_of // 2 * 2:2], mixed[1:number_of // 2 * 2:2]
    slack = jnp.minimum(lengths[source_of] - 1, bound - lengths[sink]) // 2
    slack = jnp.where((source_of == sequence[0]) | (sink == sequence[0]) | (lengths[sink] == 0), 0, jnp.maximum(slack, 0))
    shifted = jax.random.randint(jax.random.fold_in(own, 4), (number_of // 2,), 0, 1 << 20) % (slack + 1)
    lengths = lengths.at[source_of].add(-shifted).at[sink].add(shifted)
    items = jnp.searchsorted(jnp.cumsum(lengths), jnp.arange(rows * top), side="right").astype(jnp.int32)
    grid = items.reshape(top, rows).T
    grid = grid[jax.random.permutation(jax.random.fold_in(own, 1), rows)]
    turn = jax.random.randint(jax.random.fold_in(own, 2), (rows, 1), 0, top)
    return jnp.take_along_axis(grid, (jnp.arange(top)[None, :] + turn) % top, axis=1)


def shares(number_of, total, limit, skew, full):
    portions = [(1 << 20) // math.isqrt(rank ** skew) + 1 for rank in range(1, number_of + 1)]
    largest = limit if full else min(limit, max(-(-total // number_of), total * portions[0] // sum(portions)))
    least = 1 if total - largest >= number_of - 1 else 0
    holding, rest = [largest] + [least] * (number_of - 1), total - largest - least * (number_of - 1)
    while rest > 0:
        free = [i for i in range(1, number_of) if holding[i] < largest] or [i for i in range(1, number_of) if holding[i] < limit]
        whole, budget = sum([portions[i] for i in free]), rest
        for i in free:
            more = min(limit - holding[i], max(1, budget * portions[i] // whole), rest)
            holding[i] = holding[i] + more
            rest = rest - more
    return np.array(holding)


def bell_draw(stream_key, dims, scale, bound, cuts=(), kind=jnp.bfloat16):
    gain = steps_of(stream_key, dims, cuts, -0.22, 0.18) if cuts else 1.0
    entries = jax.random.normal(stream_key, dims, jnp.float32) * scale * gain
    return jnp.minimum(jnp.maximum(entries, -bound), bound).astype(kind)


def setup_inputs(seed: int = 0) -> dict:
    streams_of = jax.random.split(jax.random.key(seed), 12)
    populations = jnp.clip(1.0 + 0.1 * jax.random.normal(streams_of[0], (Q, NX, NY, NZ), jnp.float32), 0.5, 1.5)
    coarse_state = bell_draw(streams_of[1], (4, NX // 2, NY // 2, NZ // 2), 1.0, 3.0, ((1, 16), (2, 8)), jnp.float32)
    window_shift = jax.random.randint(streams_of[2], (1,), 1, N_GX).astype(jnp.int32)
    inflow = bell_draw(streams_of[3], (3,), 0.05, 0.2, (), jnp.float32)
    relaxation = jnp.clip(jax.random.uniform(streams_of[4], (1,), jnp.float32, 1.0, 1.7), 1.0, 1.7)
    positions = jnp.clip(0.25 + 6.5 * jax.random.uniform(streams_of[5], (CELLS, 3, V), jnp.float32) ** steps_of(streams_of[5], (CELLS, 3, V), ((0, 128),), -0.2, 0.2), 0.25, 6.75)
    rest_shape = bell_draw(streams_of[6], (3, V), 1.5, 6.0, (), jnp.float32)
    stiffness = jnp.clip(jnp.exp(math.log(1.0) - 2.3025851 * jax.random.uniform(streams_of[7], (CELLS,), jnp.float32) ** steps_of(streams_of[7], (CELLS,), ((0, 128),), -0.2, 0.2)), 0.1, 1.0)
    cell_owner_keys = jax.random.split(jax.random.fold_in(streams_of[8], 1), CELLS // CELLS_DEV)
    cell_owner_turns = jax.random.permutation(jax.random.fold_in(streams_of[8], 3), CELLS // CELLS_DEV)
    cell_owner = jax.vmap(lambda own, number: deal_out(jax.random.fold_in(streams_of[8], 2), own, number, CELLS_DEV, N_GX, 1, CAP, 2))(cell_owner_keys, cell_owner_turns).reshape((CELLS, 1))
    cell_block = touch_ends(jax.random.randint(streams_of[9], (CELLS,), 0, NB_DEV), jax.random.fold_in(streams_of[9], 1), 0, NB_DEV - 1).astype(jnp.int32)
    triangles = draw_triangles(jax.random.fold_in(streams_of[11], 71), 0)
    return dict(populations=populations, coarse_state=coarse_state, window_shift=window_shift, inflow=inflow, relaxation=relaxation, positions=positions, rest_shape=rest_shape, stiffness=stiffness, cell_owner=cell_owner, cell_block=cell_block, triangles=triangles)


LATTICE = ((0, 0, 0), (1, 0, 0), (-1, 0, 0), (0, 1, 0), (0, -1, 0), (0, 0, 1), (0, 0, -1),
           (1, 1, 0), (-1, -1, 0), (1, -1, 0), (-1, 1, 0), (1, 0, 1), (-1, 0, -1), (1, 0, -1), (-1, 0, 1),
           (0, 1, 1), (0, -1, -1), (0, 1, -1), (0, -1, 1))
WEIGHTS = (1.0 / 3.0,) + (1.0 / 18.0,) * 6 + (1.0 / 36.0,) * 12
COUPLING = 0.001
VELOCITY_UNIT = 20.0
HIGHEST = lax.Precision.HIGHEST


def equilibrium(density, velocity):
    square = velocity[0] * velocity[0] + velocity[1] * velocity[1] + velocity[2] * velocity[2]
    rows = []
    for along_x, along_y, along_z in LATTICE:
        project = along_x * velocity[0] + along_y * velocity[1] + along_z * velocity[2]
        rows.append(density * (1.0 + 3.0 * project + 4.5 * project * project - 1.5 * square))
    return jnp.stack(rows)


def moments(state):
    density = WEIGHTS[0] * state[0]
    for column in range(1, 19):
        density = density + WEIGHTS[column] * state[column]
    momentum = []
    for axis_id in range(3):
        total = jnp.zeros_like(density)
        for column in range(19):
            if LATTICE[column][axis_id] != 0:
                total = total + (WEIGHTS[column] * LATTICE[column][axis_id]) * state[column]
        momentum.append(total)
    return density, jnp.stack(momentum) / density


def hat_weights(point):
    nodes = jnp.arange(BS).astype(point.dtype)
    factors = [jnp.maximum(0.0, 1.0 - jnp.abs(point[axis_id][:, None] - nodes[None, :])) for axis_id in range(3)]
    joined = factors[0][:, :, None, None] * factors[1][:, None, :, None] * factors[2][:, None, None, :]
    return joined.reshape(point.shape[1], BS * BS * BS)


def laplacian(triangles, count):
    vertices = jnp.arange(count, dtype=jnp.int32)
    ends = [(triangles[:, corner][:, None] == vertices[None, :]).astype(jnp.float32) for corner in range(3)]
    total = jnp.zeros((count, count), jnp.float32)
    for first, second in ((0, 1), (1, 2), (2, 0)):
        edge = ends[second] - ends[first]
        total = total + jnp.dot(edge.T, edge, precision=HIGHEST)
    return total


def lattice_step(state, force, omega, ghost):
    density, velocity = moments(state)
    target = equilibrium(density, velocity)
    extent_x, extent_y = state.shape[1], state.shape[2]
    places_x = jnp.arange(extent_x + 2)
    places_y = jnp.arange(extent_y + 2)
    outside = ((places_x == 0) | (places_x == extent_x + 1))[:, None] | ((places_y == 0) | (places_y == extent_y + 1))[None, :]
    rows = []
    for column in range(19):
        along_x, along_y, along_z = LATTICE[column]
        push = 3.0 * (along_x * force[0] + along_y * force[1] + along_z * force[2])
        post = state[column] - omega * (state[column] - target[column]) + push
        padded = jnp.pad(post, ((1, 1), (1, 1), (0, 0)))
        padded = jnp.where(outside[:, :, None], ghost[column], padded)
        moved = padded[1 - along_x:1 - along_x + extent_x, 1 - along_y:1 - along_y + extent_y, :]
        rows.append(jnp.roll(moved, along_z, axis=2))
    return jnp.stack(rows)


def reference(populations, coarse_state, window_shift, inflow, relaxation, positions, rest_shape, stiffness, cell_owner, cell_block, triangles):
    extent_x = populations.shape[1]
    shift_rows = (window_shift[0] * CX).astype(jnp.int32)
    moved = jnp.roll(populations, -shift_rows, axis=1)
    coarse = jnp.repeat(jnp.repeat(jnp.repeat(coarse_state, 2, 1), 2, 2), 2, 3)
    fill = equilibrium(1.0 + 0.1 * coarse[0], 0.05 * coarse[1:4])
    entering = jnp.arange(extent_x, dtype=jnp.int32) + shift_rows >= extent_x
    state = jnp.where(entering[None, :, None, None], fill, moved)

    lap = laplacian(triangles, positions.shape[2])
    shape_gap = positions - rest_shape[None]
    forces = -stiffness[:, None, None] * jnp.einsum("cdv,vw->cdw", shape_gap, lap, precision=HIGHEST)

    cell_count = positions.shape[0]
    rows_y = ((jnp.arange(cell_count, dtype=jnp.int32) // CELLS_DEV) % N_GY).astype(jnp.int32)
    blocks_y = CY // BS
    blocks_z = CZ // BS
    zero = jnp.zeros((), jnp.int32)

    def anchor(owner, block, row):
        start_x = (owner * CX + block // (blocks_y * blocks_z) * BS).astype(jnp.int32)
        start_y = (row * CY + block // blocks_z % blocks_y * BS).astype(jnp.int32)
        start_z = (block % blocks_z * BS).astype(jnp.int32)
        return start_x, start_y, start_z

    def spread(field, item):
        point, push, owner, block, row = item
        local = jnp.dot(push, hat_weights(point), precision=HIGHEST).reshape(3, BS, BS, BS)
        start_x, start_y, start_z = anchor(owner, block, row)
        current = lax.dynamic_slice(field, (zero, start_x, start_y, start_z), (3, BS, BS, BS))
        return lax.dynamic_update_slice(field, current + local, (zero, start_x, start_y, start_z)), None

    empty = jnp.zeros((3,) + populations.shape[1:], jnp.float32)
    field, _ = lax.scan(spread, empty, (positions, forces, cell_owner[:, 0], cell_block, rows_y))
    force = COUPLING * field

    ghost = equilibrium(1.0, inflow)
    omega = relaxation[0]
    for repeat in range(2):
        state = lattice_step(state, force, omega, ghost)
    _, velocity = moments(state)

    def sample(carry, item):
        point, owner, block, row = item
        start_x, start_y, start_z = anchor(owner, block, row)
        local = lax.dynamic_slice(velocity, (zero, start_x, start_y, start_z), (3, BS, BS, BS)).reshape(3, BS * BS * BS)
        return carry, VELOCITY_UNIT * jnp.dot(local, hat_weights(point).T, precision=HIGHEST)

    _, cell_velocity = lax.scan(sample, zero, (positions, cell_owner[:, 0], cell_block, rows_y))
    return state, cell_velocity
```

```python
import jax
import jax.numpy as jnp
from jax import lax
from jax.experimental import pallas as pl
from jax.experimental.pallas import tpu as pltpu
from jax.sharding import PartitionSpec as P

F32 = jnp.float32
BF16 = jnp.bfloat16
Q = 19
CELLS = 16
VPAD = 768
TCHUNK = 256

LATTICE = (
    (0, 0, 0),
    (1, 0, 0),
    (-1, 0, 0),
    (0, 1, 0),
    (0, -1, 0),
    (0, 0, 1),
    (0, 0, -1),
    (1, 1, 0),
    (-1, -1, 0),
    (1, -1, 0),
    (-1, 1, 0),
    (1, 0, 1),
    (-1, 0, -1),
    (1, 0, -1),
    (-1, 0, 1),
    (0, 1, 1),
    (0, -1, -1),
    (0, 1, -1),
    (0, -1, 1),
)
W0, W1, W2 = 1.0 / 3.0, 1.0 / 18.0, 1.0 / 36.0
COUPLING = 0.001
VELOCITY_UNIT = 20.0


def having(axis, sign):
    return [q for q in range(Q) if LATTICE[q][axis] == sign]


XP, X0, XM = having(0, 1), having(0, 0), having(0, -1)
YP, Y0, YM = having(1, 1), having(1, 0), having(1, -1)
XHI, XLO = XP + X0, XM + X0
YHI, YLO = YP + Y0, YM + Y0
MSG = 22

VM = pl.BlockSpec(memory_space=pltpu.VMEM)
SM = pl.BlockSpec(memory_space=pltpu.SMEM)


def shaped(*dims, dtype=F32):
    return jax.ShapeDtypeStruct(dims, dtype)


def call(kernel, outs, specs, scratch=(), flops=10**7, name=None):
    return pl.pallas_call(
        kernel,
        out_shape=outs,
        in_specs=specs,
        out_specs=jax.tree.map(lambda _: VM, outs),
        scratch_shapes=scratch,
        cost_estimate=pl.CostEstimate(flops=flops, bytes_accessed=4 * 10**6, transcendentals=0),
        compiler_params=pltpu.CompilerParams(vmem_limit_bytes=48 * 2**20),
        name=name,
    )


def split2(x):
    high = x.astype(BF16)
    return high, (x - high.astype(F32)).astype(BF16)


def split3(x):
    high = x.astype(BF16)
    rest = x - high.astype(F32)
    middle = rest.astype(BF16)
    return high, middle, (rest - middle.astype(F32)).astype(BF16)


def thirds(x):
    n = x.shape[0] // 3
    return x[:n] + x[n : 2 * n] + x[2 * n :]


def mxu(a, b, ca=1, cb=0):
    return lax.dot_general(a, b, (((ca,), (cb,)), ((), ())), preferred_element_type=F32)


def paired(vx, vy, vz):
    return {
        1: vx, 3: vy, 5: vz, 7: vx + vy, 9: vx - vy,
        11: vx + vz, 13: vx - vz, 15: vy + vz, 17: vy - vz,
    }


def equilibrium(rho, ux, uy, uz):
    base = 1.0 - 1.5 * (ux * ux + uy * uy + uz * uz)
    rows = [None] * Q
    rows[0] = rho * base
    for q, p in paired(ux, uy, uz).items():
        even = base + 4.5 * p * p
        odd = 3.0 * p
        rows[q] = rho * (even + odd)
        rows[q + 1] = rho * (even - odd)
    return rows


def macroscopic(g):
    d = {q: g[q] - g[q + 1] for q in range(1, Q, 2)}
    s = {q: g[q] + g[q + 1] for q in range(1, Q, 2)}
    rho = W0 * g[0] + W1 * (s[1] + s[3] + s[5])
    rho = rho + W2 * ((s[7] + s[9]) + (s[11] + s[13]) + (s[15] + s[17]))
    mx = W1 * d[1] + W2 * ((d[7] + d[9]) + (d[11] + d[13]))
    my = W1 * d[3] + W2 * ((d[7] - d[9]) + (d[15] + d[17]))
    mz = W1 * d[5] + W2 * ((d[11] - d[13]) + (d[15] - d[17]))
    inverse = 1.0 / rho
    return rho, mx * inverse, my * inverse, mz * inverse


def collide(g, force, omega):
    target = equilibrium(*macroscopic(g))
    post = [g[q] - omega * (g[q] - target[q]) for q in range(Q)]
    for q, p in paired(*(3.0 * f for f in force)).items():
        post[q] = post[q] + p
        post[q + 1] = post[q + 1] - p
    return post


def hat(row, nodes):
    return jnp.maximum(0.0, 1.0 - jnp.abs(row - nodes))


def planar(pos_ref, c, nodes):
    wx = hat(pos_ref[0, pl.ds(c, 1), :], nodes)
    wy = hat(pos_ref[1, pl.ds(c, 1), :], nodes)
    wz = hat(pos_ref[2, pl.ds(c, 1), :], nodes)
    return jnp.concatenate([wx[n : n + 1] * wy for n in range(8)], axis=0), wz


def zero_counts(count_s):
    for i in range(CELLS):
        count_s[i] = 0


def next_slot(owner_s, count_s, c):
    o = owner_s[c]
    r = count_s[o]
    count_s[o] = r + 1
    return o, r


def cell_kernel(owner_s, block_s, pos_ref, rest_ref, stiff_ref, tri_ref, out_ref, acc_s, count_s):
    gap = (pos_ref[...] - rest_ref[...][:, None, :]).reshape(48, VPAD)
    pieces = jnp.concatenate(split3(gap), axis=0)
    acc_s[...] = jnp.zeros_like(acc_s)
    vertex = lax.broadcasted_iota(jnp.int32, (VPAD, TCHUNK), 0)

    def chunk(i, carry):
        tri = tri_ref[:, pl.ds(pl.multiple_of(i * TCHUNK, TCHUNK), TCHUNK)]
        ends = [
            jnp.where(tri[k : k + 1, :] == vertex, 1.0, 0.0).astype(BF16) for k in range(3)
        ]
        at = [thirds(mxu(pieces, ends[k])) for k in range(3)]
        total = acc_s[...]
        for k in range(3):
            pull = (at[k] - at[(k + 1) % 3]) + (at[k] - at[(k + 2) % 3])
            total = total + thirds(mxu(jnp.concatenate(split3(pull), axis=0), ends[k], 1, 1))
        acc_s[...] = total
        return carry

    lax.fori_loop(0, tri_ref.shape[1] // TCHUNK, chunk, 0)
    acc_s[...] = (-stiff_ref[...][None] * acc_s[...].reshape(3, CELLS, VPAD)).reshape(48, VPAD)

    nodes = lax.broadcasted_iota(jnp.int32, (8, VPAD), 0).astype(F32)
    half = lax.broadcasted_iota(jnp.int32, (32, 128), 1) // 64
    zero_counts(count_s)
    blank = jnp.concatenate([jnp.zeros((24, 128), F32), jnp.full((8, 128), -1.0, F32)], axis=0)
    for o in range(CELLS):
        out_ref[o] = blank

    def cell(c, carry):
        plane, wz = planar(pos_ref, c, nodes)
        rows = [acc_s[pl.ds(d * CELLS + c, 1), :] * wz for d in range(3)]
        a_high, a_low = split2(jnp.concatenate(rows + [jnp.zeros_like(wz)], axis=0))
        b_high, b_low = split2(plane)
        both = mxu(jnp.concatenate([a_high, a_low], axis=0), b_high, 1, 1)
        res = (both[:24] + both[32:56]) + mxu(a_high, b_low, 1, 1)[:24]
        full = jnp.concatenate([res, jnp.full((8, 64), block_s[c].astype(F32), F32)], axis=0)
        full = jnp.concatenate([full, full], axis=1)
        o, r = next_slot(owner_s, count_s, c)
        out_ref[o] = jnp.where(half == r, full, out_ref[o])
        return carry

    lax.fori_loop(0, CELLS, cell, 0)


def field_kernel(arrived_ref, coarse_ref, force_ref, match_ref, coarse_out_ref):
    col = lax.broadcasted_iota(jnp.int32, (128, 512), 1)
    block = ((col // 128) * 16 + (col % 128) // 8).astype(F32)
    same = col % 8 == lax.broadcasted_iota(jnp.int32, (128, 512), 0) % 8
    tags = arrived_ref[:, 24:32, :].reshape(128, 128)
    match = jnp.concatenate(
        [
            jnp.where(same & (tags[:, 64 * j : 64 * j + 1] == block), 1.0, 0.0).astype(BF16)
            for j in range(2)
        ],
        axis=0,
    )
    match_ref[...] = match
    sides = []
    for d in range(3):
        flipped = arrived_ref[:, 8 * d : 8 * d + 8, :].reshape(128, 128).T
        sides.append(jnp.concatenate([flipped[:64], flipped[64:]], axis=1))
    placed = thirds(mxu(jnp.concatenate(split3(jnp.concatenate(sides, axis=0)), axis=0), match))
    for d in range(3):
        for bx in range(2):
            for by in range(2):
                k = bx * 2 + by
                tile = placed[64 * d : 64 * d + 64, 128 * k : 128 * k + 128]
                force_ref[d, 8 * bx : 8 * bx + 8, 8 * by : 8 * by + 8, :] = (
                    COUPLING * tile
                ).reshape(8, 8, 128)
    fine = lax.broadcasted_iota(jnp.int32, (64, 128), 1) // 2
    repeat = jnp.where(fine == lax.broadcasted_iota(jnp.int32, (64, 128), 0), 1.0, 0.0)
    parts = jnp.concatenate(split3(coarse_ref[...]), axis=0)
    coarse_out_ref[...] = thirds(mxu(parts, repeat.astype(BF16)))


def turn_kernel(index_ref, in_ref, out_ref):
    out_ref[...] = in_ref[...]


def turned(received, index):
    block = (1,) + received.shape[1:]
    return pl.pallas_call(
        turn_kernel,
        out_shape=jax.ShapeDtypeStruct(received.shape, received.dtype),
        grid_spec=pltpu.PrefetchScalarGridSpec(
            num_scalar_prefetch=1,
            grid=(received.shape[0],),
            in_specs=[pl.BlockSpec(block, lambda i, index: (index[i], 0, 0, 0))],
            out_specs=pl.BlockSpec(block, lambda i, index: (i, 0, 0, 0)),
        ),
        name="turn",
    )(index, received)


def first_kernel(
    ints, floats, state_ref, coarse_ref, force_ref, post_ref, xh_ref, xl_ref, yh_ref, yl_ref
):
    omega = floats[0]
    fill = ints[0] == 1

    def plane(x, carry):
        c = [coarse_ref[k, x // 2] for k in range(4)]
        fresh = equilibrium(1.0 + 0.1 * c[0], 0.05 * c[1], 0.05 * c[2], 0.05 * c[3])
        g = [jnp.where(fill, fresh[q], state_ref[q, x]) for q in range(Q)]
        force = [force_ref[d, x] for d in range(3)]
        post = collide(g, force, omega)
        for q in range(Q):
            post_ref[q, x] = post[q]
        for ref, near, far, order, first in (
            (yh_ref, 15, 14, YHI, YP),
            (yl_ref, 0, 1, YLO, YM),
        ):
            rows = [post[q][near : near + 1] for q in order]
            rows += [post[q][far : far + 1] for q in first]
            rows += [force[d][near : near + 1] for d in range(3)]
            for k in range(MSG):
                ref[k, pl.ds(x, 1), :] = rows[k]
        return carry

    lax.fori_loop(0, 16, plane, 0)
    for ref, near, far, order, first in ((xh_ref, 15, 14, XHI, XP), (xl_ref, 0, 1, XLO, XM)):
        for k, q in enumerate(order):
            ref[k] = post_ref[q, near]
        for k, q in enumerate(first):
            ref[14 + k] = post_ref[q, far]
        for d in range(3):
            ref[19 + d] = force_ref[d, near]


def widen_kernel(ints, floats, own_h, own_l, from_lo, from_hi, out_h, out_l):
    low, high = ints[1] == 1, ints[2] == 1
    for own, out, near, far, order, first in (
        (own_h, out_h, 15, 14, YHI, YP),
        (own_l, out_l, 0, 1, YLO, YM),
    ):
        for k in range(MSG):
            out[k, 2:18, :] = own[k]
            if k >= 19:
                out[k, 1:2, :] = from_lo[k, near : near + 1, :]
                out[k, 18:19, :] = from_hi[k, near : near + 1, :]
                continue
            q, row = (order[k], near) if k < 14 else (first[k - 14], far)
            ghost = floats[1 + q]
            for at, source, side, names, deep in (
                (1, from_lo, low, XHI, 0),
                (0, from_lo, low, XP, 14),
                (18, from_hi, high, XLO, 0),
                (19, from_hi, high, XM, 14),
            ):
                if q in names:
                    value = source[deep + names.index(q), row : row + 1, :]
                    out[k, at : at + 1, :] = jnp.where(side, ghost, value)


def second_kernel(
    ints, floats, post_ref, force_ref, match_ref,
    from_xlo, from_xhi, own_yh, own_yl, from_ylo, from_yhi,
    flow_ref, back_ref, wide_s, push_s, next_s, lo_s, hi_s, speed_s,
):
    omega = floats[0]
    low_x, high_x, low_y, high_y = (ints[k] == 1 for k in range(1, 5))
    for q in range(Q):
        ghost = floats[1 + q]
        for at, source, side, names, deep in (
            (1, from_xlo, low_x, XHI, 0),
            (0, from_xlo, low_x, XP, 14),
            (18, from_xhi, high_x, XLO, 0),
            (19, from_xhi, high_x, XM, 14),
        ):
            if q in names:
                wide_s[q, at] = jnp.where(side, ghost, source[deep + names.index(q)])
    for d in range(3):
        push_s[d, 0] = from_xlo[19 + d]
        push_s[d, 17] = from_xhi[19 + d]

    def copy(x, carry):
        for q in range(Q):
            wide_s[q, x + 2] = post_ref[q, x]
        for d in range(3):
            push_s[d, x + 1] = force_ref[d, x]
        return carry

    lax.fori_loop(0, 16, copy, 0)
    row = lax.broadcasted_iota(jnp.int32, (16, 128), 0)
    top, bottom = row == 15, row == 0

    def around(v, q):
        cz = LATTICE[q][2]
        return v if cz == 0 else pltpu.roll(v, cz % 128, 1)

    def across(v, q, below, above):
        cy = LATTICE[q][1]
        if cy == 1:
            return jnp.where(bottom, below(), pltpu.roll(v, 1, 0))
        if cy == -1:
            return jnp.where(top, above(), pltpu.roll(v, 15, 0))
        return v

    def plane(xe, carry):
        g = []
        for q in range(Q):
            at = xe + 1 - LATTICE[q][0]
            ghost = floats[1 + q]

            def below():
                return jnp.where(low_y, ghost, from_ylo[YHI.index(q), pl.ds(at, 1), :])

            def above():
                return jnp.where(high_y, ghost, from_yhi[YLO.index(q), pl.ds(at, 1), :])

            g.append(around(across(wide_s[q, at], q, below, above), q))
        post = collide(g, [push_s[d, xe] for d in range(3)], omega)
        outside = ((xe == 0) & low_x) | ((xe == 17) & high_x)
        for q in range(Q):
            next_s[q, xe] = around(jnp.where(outside, floats[1 + q], post[q]), q)
        return carry

    lax.fori_loop(0, 18, plane, 0)

    places = lax.broadcasted_iota(jnp.int32, (18, 128), 0)
    outside_x = ((places == 0) & low_x) | ((places == 17) & high_x)
    for keep, side, come, own, order, first, mine, leaving in (
        (lo_s, low_y, from_ylo, own_yl, YHI, YP, YLO, YP),
        (hi_s, high_y, from_yhi, own_yh, YLO, YM, YHI, YM),
    ):
        g = []
        for q in range(Q):
            start = 1 - LATTICE[q][0]
            if q in first:
                source, k = come, 14 + first.index(q)
            elif q in order:
                source, k = come, order.index(q)
            else:
                source, k = own, mine.index(q)
            g.append(around(source[k, start : start + 18, :], q))
        post = collide(g, [come[19 + d, 1:19, :] for d in range(3)], omega)
        for k, q in enumerate(leaving):
            keep[k, 0:18, :] = around(jnp.where(outside_x | side, floats[1 + q], post[q]), q)

    def finish(x, carry):
        g = []
        for q in range(Q):
            at = x + 1 - LATTICE[q][0]

            def below():
                return lo_s[YP.index(q), pl.ds(at, 1), :]

            def above():
                return hi_s[YM.index(q), pl.ds(at, 1), :]

            v = across(next_s[q, at], q, below, above)
            flow_ref[q, x] = v
            g.append(v)
        speed = macroscopic(g)
        for d in range(3):
            speed_s[d, x] = speed[1 + d]
        return carry

    lax.fori_loop(0, 16, finish, 0)
    rows = []
    for d in range(3):
        tiles = [
            speed_s[d, 8 * bx : 8 * bx + 8, 8 * by : 8 * by + 8, :].reshape(64, 128)
            for bx in range(2)
            for by in range(2)
        ]
        rows.append(jnp.concatenate(tiles, axis=1))
    parts = jnp.concatenate(split3(jnp.concatenate(rows, axis=0)), axis=0)
    got = mxu(match_ref[...], parts, 1, 1)
    got = got[:, :192] + got[:, 192:384] + got[:, 384:]
    for d in range(3):
        pair = jnp.concatenate(
            [got[:128, 64 * d : 64 * d + 64], got[128:, 64 * d : 64 * d + 64]], axis=1
        )
        back_ref[:, 8 * d : 8 * d + 8, :] = pair.reshape(16, 8, 128)


def sample_kernel(owner_s, pos_ref, back_ref, out_ref, count_s):
    nodes = lax.broadcasted_iota(jnp.int32, (8, VPAD), 0).astype(F32)
    zero_counts(count_s)

    def cell(c, carry):
        plane, wz = planar(pos_ref, c, nodes)
        o, r = next_slot(owner_s, count_s, c)
        local = back_ref[o]
        local = jnp.where(r == 0, local[:, :64], local[:, 64:])
        local = jnp.concatenate([local, jnp.zeros((8, 64), F32)], axis=0)
        a_high, a_low = split2(local)
        b_high, b_low = split2(plane)
        both = mxu(jnp.concatenate([a_high, a_low], axis=0), b_high)
        got = (both[:24] + both[32:56]) + mxu(a_high, b_low)[:24]
        rows = [
            jnp.sum(got[8 * d : 8 * d + 8] * wz, axis=0, keepdims=True) for d in range(3)
        ]
        out_ref[c] = VELOCITY_UNIT * jnp.concatenate(rows, axis=0)[:, : out_ref.shape[2]]
        return carry

    lax.fori_loop(0, CELLS, cell, 0)


def shifts(count):
    up = [(i, i + 1) for i in range(count - 1)]
    return up, [(b, a) for a, b in up]


def swap(x):
    return lax.all_to_all(x, "gx", split_axis=0, concat_axis=0, tiled=True)


def body(
    populations,
    coarse_state,
    window_shift,
    inflow,
    relaxation,
    positions,
    rest_shape,
    stiffness,
    cell_owner,
    cell_block,
    triangles,
):
    span_x = lax.axis_size("gx")
    span_y = lax.axis_size("gy")
    here_x = lax.axis_index("gx")
    here_y = lax.axis_index("gy")
    step = window_shift[0]
    owner = cell_owner[:, 0]
    vertices = positions.shape[2]

    ghost = jnp.stack(equilibrium(1.0, inflow[0], inflow[1], inflow[2]))
    floats = jnp.concatenate([relaxation, ghost])
    ints = jnp.stack(
        [
            here_x + step >= span_x,
            here_x == 0,
            here_x == span_x - 1,
            here_y == 0,
            here_y == span_y - 1,
        ]
    ).astype(jnp.int32)

    spread = swap(populations.reshape(16, Q, 16, 128))
    index = jnp.minimum(jnp.arange(16, dtype=jnp.int32) + step, 15)

    pos = jnp.pad(positions.transpose(1, 0, 2), ((0, 0), (0, 0), (0, VPAD - vertices)))
    rest = jnp.pad(rest_shape, ((0, 0), (0, VPAD - vertices)))
    outgoing = call(
        cell_kernel,
        shaped(16, 32, 128),
        [SM, SM, VM, VM, VM, VM],
        [pltpu.VMEM((48, VPAD), F32), pltpu.SMEM((CELLS,), jnp.int32)],
        name="cells",
    )(owner, cell_block, pos, rest, stiffness[:, None], triangles.T)
    arrived = swap(outgoing)
    coarse = jnp.repeat(coarse_state, 2, axis=2).reshape(512, 64)
    force, match, coarse = call(
        field_kernel,
        (shaped(3, 16, 16, 128), shaped(256, 512, dtype=BF16), shaped(512, 128)),
        [VM, VM],
        name="field",
    )(arrived, coarse)

    state = swap(turned(spread, index)).reshape(Q, 16, 16, 128)

    half = shaped(MSG, 16, 128)
    post, xh, xl, yh, yl = call(
        first_kernel,
        (shaped(Q, 16, 16, 128), half, half, half, half),
        [SM, SM, VM, VM, VM],
        name="first",
    )(ints, floats, state, coarse.reshape(4, 8, 16, 128), force)
    up, down = shifts(span_x)
    from_xlo = lax.ppermute(xh, "gx", up)
    from_xhi = lax.ppermute(xl, "gx", down)
    wide = shaped(MSG, 20, 128)
    own_yh, own_yl = call(
        widen_kernel, (wide, wide), [SM, SM, VM, VM, VM, VM], name="widen"
    )(ints, floats, yh, yl, from_xlo, from_xhi)
    up, down = shifts(span_y)
    from_ylo = lax.ppermute(own_yh, "gy", up)
    from_yhi = lax.ppermute(own_yl, "gy", down)
    flow, back = call(
        second_kernel,
        (shaped(Q, 16, 16, 128), shaped(16, 24, 128)),
        [SM, SM] + [VM] * 9,
        [
            pltpu.VMEM((Q, 20, 16, 128), F32),
            pltpu.VMEM((3, 18, 16, 128), F32),
            pltpu.VMEM((Q, 18, 16, 128), F32),
            pltpu.VMEM((5, 24, 128), F32),
            pltpu.VMEM((5, 24, 128), F32),
            pltpu.VMEM((3, 16, 16, 128), F32),
        ],
        name="second",
    )(ints, floats, post, force, match, from_xlo, from_xhi, own_yh, own_yl, from_ylo, from_yhi)
    cell_velocity = call(
        sample_kernel,
        shaped(CELLS, 3, vertices),
        [SM, VM, VM],
        [pltpu.SMEM((CELLS,), jnp.int32)],
        name="sample",
    )(owner, pos, swap(back))
    return flow, cell_velocity


def solution(mesh):
    placed = (
        P(None, "gx", "gy", None),
        P(None, "gx", "gy", None),
        P(),
        P(),
        P(),
        P(("gx", "gy"), None, None),
        P(),
        P(("gx", "gy")),
        P(("gx", "gy"), None),
        P(("gx", "gy")),
        P(),
    )
    return jax.shard_map(
        body,
        mesh=mesh,
        in_specs=placed,
        out_specs=(P(None, "gx", "gy", None), P(("gx", "gy"), None, None)),
        check_vma=False,
    )
```
